512 devices in a mesh: inb: 16 (over y, z_lo), hid: 32 (over z_hi, x, core).
Axes of the slice: x: 4, y: 4, z: 16 (z_hi: 4, z_lo: 4; z = z_hi * 4 + z_lo), core: 2. Of those that a mesh axis runs over, the one named last changes fastest.
Arguments:
- activations: bfloat16 [2, 512, 16384], P(None, 'hid', 'inb'), may hold values from -40 to 40
- out_grads: bfloat16 [2, 512, 32768], P(None, 'inb', 'hid'), may hold values from -1 to 1
- basis_in: bfloat16 [16384, 1024], P('inb', 'hid'), may hold values from -0.1875 to 0.1875
- basis_out: bfloat16 [32768, 1024], P('hid', 'inb'), may hold values from -0.1875 to 0.1875
Outputs:
- precond: bfloat16 [16384, 32768], P('inb', 'hid')
The draws below stay inside these ranges and needn't reach their ends.
All inputs are finite; a program needn't handle non-finite values.
Results may differ from the reference program's by a relative error of at most 0.0058.
Values may be sent and summed in bfloat16 or wider, within the bound.
A program may use at most 64 MiB of HBM per device.

```python
import math
import jax
import jax.numpy as jnp
from jax import lax

BLOCK = 1024
MICRO = 2
MB_TOK = 512
IN = 16384
HID = 32768


def token_levels(key):
    level = jax.random.uniform(jax.random.fold_in(key, 4242), (MICRO, MB_TOK), jnp.float32)
    return 10.0 ** (level - 0.5)


def draw_activations(key, part):
    row_scale = token_levels(key)
    column_scale = 10.0 ** (jax.random.uniform(jax.random.fold_in(key, 17), (IN,), jnp.float32) - 0.5)
    noise_key = jax.random.fold_in(key, 23)
    noise = jax.random.truncated_normal(noise_key, -4.0, 4.0, (MICRO, MB_TOK, IN), jnp.float32)
    values = noise * row_scale[:, :, None] * column_scale[None, None, :]
    return jnp.clip(values, -40.0, 40.0).astype(jnp.bfloat16)


def draw_out_grads(key, part):
    row_scale = token_levels(key)
    overall = 0.2 / math.sqrt(MICRO * MB_TOK)
    noise_key = jax.random.fold_in(key, 31)
    noise = jax.random.truncated_normal(noise_key, -4.0, 4.0, (MICRO, MB_TOK, HID), jnp.float32)
    values = noise * row_scale[:, :, None] * overall
    return jnp.clip(values, -1.0, 1.0).astype(jnp.bfloat16)


def levels(key, shape, pieces, least, largest):
    loudness = 1.0
    for position, parts in pieces:
        heights = jax.random.uniform(jax.random.fold_in(jax.random.fold_in(key, 6), position), (parts,), jnp.float32, least / len(pieces), largest / len(pieces))
        loudness = loudness * jnp.repeat(jnp.exp(heights), shape[position] // parts).reshape((-1,) + (1,) * (len(shape) - 1 - position))
    return loudness


def gaussian(own_key, extent, spread, most, split=(), held_as=jnp.bfloat16):
    entries = spread * jax.random.normal(own_key, extent, jnp.float32)
    if split:
        entries = entries * levels(own_key, extent, split, -0.22, 0.18)
    return jnp.clip(entries, -most, most).astype(held_as)


def setup_inputs(seed: int = 0) -> dict:
    seeds = jax.random.split(jax.random.key(seed), 5)
    activations = draw_activations(jax.random.fold_in(seeds[4], 71), 0)
    out_grads = draw_out_grads(jax.random.fold_in(seeds[4], 71), 0)
    basis_in = gaussian(seeds[2], (IN, BLOCK), BLOCK ** -0.5, 0.1875, ((0, 16), (1, 32)))
    basis_out = gaussian(seeds[3], (HID, BLOCK), BLOCK ** -0.5, 0.1875, ((0, 32), (1, 16)))
    return {"activations": activations, "out_grads": out_grads, "basis_in": basis_in, "basis_out": basis_out}


damping = 0.1


def rotate_all(values, basis, block_count):
    def rotate_block(number):
        offset = (number * BLOCK).astype(jnp.int32)
        segment = lax.dynamic_slice_in_dim(values, offset, BLOCK, 1)
        square_part = lax.dynamic_slice_in_dim(basis, offset, BLOCK, 0)
        return jnp.dot(segment, square_part, preferred_element_type=jnp.float32).astype(jnp.bfloat16)
    return lax.map(rotate_block, jnp.arange(block_count, dtype=jnp.int32))


def square_round(values):
    widened = values.astype(jnp.float32)
    return (widened * widened).astype(jnp.bfloat16)


def reference(activations, out_grads, basis_in, basis_out):
    total_tokens = MICRO * MB_TOK
    acts_flat = activations.reshape(total_tokens, IN)
    grads_flat = out_grads.reshape(total_tokens, HID)
    rot_in = rotate_all(acts_flat, basis_in, IN // BLOCK)
    rot_out = rotate_all(grads_flat, basis_out, HID // BLOCK)
    grad_rows = jnp.transpose(rot_out, (1, 0, 2)).reshape(total_tokens, HID)
    grad_squares = square_round(grad_rows)
    dims = (((0,), (0,)), ((), ()))

    def tile_rows(act_rot):
        act_squares = square_round(act_rot)
        grad_rot = lax.dot_general(act_rot, grad_rows, dims, preferred_element_type=jnp.float32)
        fisher = lax.dot_general(act_squares, grad_squares, dims, preferred_element_type=jnp.float32)
        return (grad_rot / (fisher + damping)).astype(jnp.bfloat16)

    tiles = lax.map(tile_rows, rot_in)
    return tiles.reshape(IN, HID)
```

```python
import functools

import jax
import jax.numpy as jnp
from jax import lax
from jax.experimental import pallas as pl
from jax.experimental.pallas import tpu as pltpu
from jax.sharding import PartitionSpec as P

damping = 0.1
MESH = pl.DeviceIdType.MESH
bf16 = jnp.bfloat16
f32 = jnp.float32


class Names:
    def __init__(self):
        self.slots = {}

    def __getitem__(self, name):
        return self.slots.setdefault(name, len(self.slots))


def square(values):
    wide = values.astype(f32)
    return (wide * wide).astype(bf16)


def nt_dot(left, right):
    return lax.dot_general(
        left, right, (((1,), (1,)), ((), ())), preferred_element_type=f32
    )


def kernel(
    acts, grads, bin_t, bout_t, out,
    TB, CB, RO, SO, TH, CH, RT, ST, load_sem, send_sem, recv_sem,
):
    inb = lax.axis_index("inb")
    hid = lax.axis_index("hid")
    y, zl = inb // 4, inb % 4
    zh, x, c = hid // 8, (hid // 2) % 4, hid % 2
    Y1, Y0, Z1, Z0 = y // 2, y % 2, zl // 2, zl % 2
    is_mid = (zl == 1) | (zl == 2)

    def flip(value, mask):
        for bit in (1, 2):
            if mask & bit:
                value = value + bit - 2 * bit * ((value // bit) % 2)
        return value

    def peer(dy=0, dzl=0, dzh=0, dx=0, dc=0):
        return (
            flip(y, dy) * 4 + flip(zl, dzl),
            flip(zh, dzh) * 8 + flip(x, dx) * 2 + flip(c, dc),
        )

    def xx(position):
        return (position % 2) * 2 + position // 2

    slots, sends = Names(), []

    def send(name, ref, whom, when=None):
        slot = slots[name]
        copy = pltpu.make_async_remote_copy(
            ref, ref, send_sem.at[len(sends)], recv_sem.at[slot],
            device_id=whom, device_id_type=MESH,
        )
        sends.append((copy, when))
        if when is None:
            copy.start()
        else:
            pl.when(when)(copy.start)

    def send_to(name, ref, target, whom):
        copy = pltpu.make_async_remote_copy(
            ref, target, send_sem.at[len(sends)], recv_sem.at[slots[name]],
            device_id=whom, device_id_type=MESH,
        )
        sends.append((copy, None))
        copy.start()

    def arrived(name, ref):
        pltpu.make_async_remote_copy(
            ref, ref, send_sem.at[0], recv_sem.at[slots[name]],
            device_id=peer(dc=1), device_id_type=MESH,
        ).wait_recv()

    t_chunk = TH.at[zh, xx(x), c]
    c_chunk = CH.at[zh, x, c]
    loads = [
        pltpu.make_async_copy(bout_t, CB.at[0, Z0], load_sem.at[0]),
        pltpu.make_async_copy(grads.at[:, pl.ds(0, 16)], TB.at[Y0, Z1, 0], load_sem.at[1]),
        pltpu.make_async_copy(grads.at[:, pl.ds(16, 16)], TB.at[Y0, Z1, 1], load_sem.at[2]),
        pltpu.make_async_copy(acts, t_chunk, load_sem.at[3]),
        pltpu.make_async_copy(bin_t, c_chunk, load_sem.at[4]),
    ]
    for load in loads:
        load.start()

    peers = [peer(dc=1)]
    peers += [peer(dx=d) for d in (1, 2, 3)]
    peers += [peer(dzh=d) for d in (1, 3)]
    peers += [peer(dy=d) for d in (1, 3)]
    peers += [peer(dzl=d) for d in (1, 2, 3)]
    barrier = pltpu.get_barrier_semaphore()
    for whom in peers:
        pl.semaphore_signal(barrier, inc=1, device_id=whom, device_id_type=MESH)
    pl.semaphore_wait(barrier, len(peers))
    for load in loads:
        load.wait()

    def th(dzh, dx=0, core=None):
        return TH.at[flip(zh, dzh), xx(flip(x, dx)), c if core is None else core]

    def ch(dzh, dx=0, core=None):
        return CH.at[flip(zh, dzh), flip(x, dx), c if core is None else core]

    def th_half(dzh, half):
        return TH.at[flip(zh, dzh), xx(x), c, half]

    def ch_half(dzh, half):
        return CH.at[flip(zh, dzh), x, c, pl.ds(16 * half, 16)]

    def ro(dy, dzl, piece):
        yy, zz = flip(y, dy), flip(zl, dzl)
        column = 2 * flip(yy, 3 * piece) + zz // 2
        return RO.at[column, yy // 2, :, zz % 2]

    def z_own(kind, chunk):
        for d in (1, 3):
            send((kind, "z", d), chunk(0), peer(dzh=d))

    def x_send(kind, chunk, dzh):
        for d in (1, 3, 2):
            send((kind, "x", dzh, d), chunk(dzh), peer(dx=d))

    def z_relay(kind, chunk, half_of):
        arrived((kind, "z", 1), chunk(1))
        send((kind, "r", 0), half_of(1, 0), peer(dzh=3))
        x_send(kind, chunk, 1)
        arrived((kind, "z", 3), chunk(3))
        send((kind, "r", 1), half_of(3, 1), peer(dzh=1))
        x_send(kind, chunk, 3)

    def z_opposite(kind, chunk, half_of):
        for half in (0, 1):
            arrived((kind, "r", half), half_of(2, half))
        x_send(kind, chunk, 2)

    def core_send(kind, chunk, whole, dzh):
        for d in (1, 3, 2):
            arrived((kind, "x", dzh, d), chunk(dzh, d))
        send((kind, "c", dzh), whole.at[flip(zh, dzh), :, c], peer(dc=1))

    def core_wait(kind, whole, dzh):
        arrived((kind, "c", dzh), whole.at[flip(zh, dzh), :, flip(c, 1)])

    send("Cz", CB.at[0, Z0], peer(dzl=1))
    send("Tz", TB.at[Y0, Z1], peer(dzl=2))
    send_to("Cy", CB.at[0, Z0], CB.at[1, Z0], peer(dy=3))
    send("Ty", TB.at[Y0, Z1], peer(dy=1))
    z_own("T", th)
    x_send("T", th, 0)
    arrived("Cz", CB.at[0, flip(Z0, 1)])
    send_to("Cy2", CB.at[0, flip(Z0, 1)], CB.at[1, flip(Z0, 1)], peer(dy=3))
    arrived("Tz", TB.at[Y0, flip(Z1, 1)])
    send("Ty2", TB.at[Y0, flip(Z1, 1)], peer(dy=1))
    z_relay("T", th, th_half)
    x_send("C", ch, 0)

    arrived("Ty", TB.at[flip(Y0, 1), Z1])
    arrived("Ty2", TB.at[flip(Y0, 1), flip(Z1, 1)])
    arrived("Cy", CB.at[1, Z0])
    arrived("Cy2", CB.at[1, flip(Z0, 1)])
    tokens = TB[...].reshape(256, 1024)
    for piece in (0, 1):
        rotated = nt_dot(tokens, CB[piece].reshape(128, 1024)).astype(bf16)
        ro(0, 0, piece)[...] = rotated.reshape(2, 128, 128)

    def y_send(dzl):
        for piece in (0, 1):
            for d in (1, 3):
                send(("Ry", dzl, piece, d), ro(0, dzl, piece), peer(dy=d))

    def y_relay(dzl):
        arrived(("Ry", dzl, 0, 1), ro(1, dzl, 0))
        send(("Rr", dzl, 0), ro(1, dzl, 0), peer(dy=3))
        arrived(("Ry", dzl, 1, 3), ro(3, dzl, 1))
        send(("Rr", dzl, 1), ro(3, dzl, 1), peer(dy=1))

    for piece in (0, 1):
        send(("Rz", 1, piece), ro(0, 0, piece), peer(dzl=1))
        send(("Rz", 3, piece), ro(0, 0, piece), peer(dzl=3), is_mid)
    y_send(0)
    z_opposite("T", th, th_half)
    z_own("C", ch)
    for piece in (0, 1):
        arrived(("Rz", 1, piece), ro(0, 1, piece))
        send(("Rz", 2, piece), ro(0, 1, piece), peer(dzl=3), is_mid)
    y_send(1)
    y_relay(0)
    for piece in (0, 1):
        arrived(("Rz", 3, piece), ro(0, 3, piece))
        send(("Rz", 2, piece), ro(0, 3, piece), peer(dzl=1), is_mid)
    for piece in (0, 1):
        arrived(("Rz", 2, piece), ro(0, 2, piece))
        send(("Rz", 3, piece), ro(0, 2, piece), peer(dzl=1), is_mid)
    y_send(3)
    y_send(2)
    y_relay(1)
    z_relay("C", ch, ch_half)
    for dzh in (0, 1, 3, 2):
        core_send("T", th, TH, dzh)
    y_relay(3)
    y_relay(2)
    z_opposite("C", ch, ch_half)
    for dzh in (0, 1, 3):
        core_send("C", ch, CH, dzh)
    for dzh in (0, 1, 3, 2):
        core_wait("T", TH, dzh)

    def rotate_plane(dzh):
        plane = flip(zh, dzh)
        columns = CH[plane].reshape(256, 1024)

        @pl.loop(0, 4)
        def _(block):
            rotated = nt_dot(columns, TH[block].reshape(256, 1024)).astype(bf16)
            RT[block] = rotated
            ST[block] = square(rotated)

    def finish_plane(dzh):
        plane = flip(zh, dzh)

        @pl.loop(0, 4)
        def _(block):
            left = jnp.concatenate([RT[i] for i in range(4)], axis=1)
            left_sq = jnp.concatenate([ST[i] for i in range(4)], axis=1)

            def right(ref):
                return jnp.concatenate(
                    [ref[2 * block + i].reshape(1024, 128) for i in (0, 1)], axis=1
                )

            grad = jnp.dot(left, right(RO), preferred_element_type=f32)
            fisher = jnp.dot(left_sq, right(SO), preferred_element_type=f32)
            rows = pl.ds(pl.multiple_of(plane * 256, 256), 256)
            lanes = pl.ds(pl.multiple_of(block * 256, 256), 256)
            out[rows, lanes] = (grad / (fisher + damping)).astype(bf16)

    core_wait("C", CH, 0)
    rotate_plane(0)
    for dzl in (0, 1, 3, 2):
        arrived(("Ry", dzl, 0, 3), ro(3, dzl, 0))
        arrived(("Ry", dzl, 1, 1), ro(1, dzl, 1))
        arrived(("Rr", dzl, 0), ro(2, dzl, 0))
        arrived(("Rr", dzl, 1), ro(2, dzl, 1))

    @pl.loop(0, 8)
    def _(column):
        SO[column] = square(RO[column])

    finish_plane(0)
    for dzh in (1, 3):
        core_wait("C", CH, dzh)
        rotate_plane(dzh)
        finish_plane(dzh)
    core_send("C", ch, CH, 2)
    core_wait("C", CH, 2)
    rotate_plane(2)
    finish_plane(2)
    for copy, when in sends:
        if when is None:
            copy.wait_send()
        else:
            pl.when(when)(copy.wait_send)


def on_device(activations, out_grads, basis_in, basis_out):
    return pl.pallas_call(
        kernel,
        out_shape=jax.ShapeDtypeStruct((1024, 1024), bf16),
        in_specs=[pl.BlockSpec(memory_space=pl.ANY)] * 4,
        out_specs=pl.BlockSpec(memory_space=pltpu.VMEM),
        scratch_shapes=[
            pltpu.VMEM((2, 2, 2, 2, 16, 1024), bf16),
            pltpu.VMEM((2, 2, 64, 1024), bf16),
            pltpu.VMEM((8, 2, 2, 2, 128, 128), bf16),
            pltpu.VMEM((8, 2, 2, 2, 128, 128), bf16),
            pltpu.VMEM((4, 4, 2, 2, 16, 1024), bf16),
            pltpu.VMEM((4, 4, 2, 32, 1024), bf16),
            pltpu.VMEM((4, 256, 256), bf16),
            pltpu.VMEM((4, 256, 256), bf16),
            pltpu.SemaphoreType.DMA((5,)),
            pltpu.SemaphoreType.DMA((128,)),
            pltpu.SemaphoreType.DMA((96,)),
        ],
        compiler_params=pltpu.CompilerParams(
            collective_id=0, has_side_effects=True, vmem_limit_bytes=48 * 2**20
        ),
        name="fused",
    )(activations, out_grads, basis_in.T, basis_out.T)


def solution(mesh):
    return jax.shard_map(
        on_device,
        mesh=mesh,
        in_specs=(P(None, "hid", "inb"), P(None, "inb", "hid"), P("inb", "hid"), P("hid", "inb")),
        out_specs=P("inb", "hid"),
        check_vma=False,
    )
```

```python
import functools

import jax
import jax.numpy as jnp
from jax import lax
from jax.experimental import pallas as pl
from jax.experimental.pallas import tpu as pltpu
from jax.sharding import PartitionSpec as P

damping = 0.1
MESH = pl.DeviceIdType.MESH
bf16 = jnp.bfloat16
f32 = jnp.float32


class Names:
    def __init__(self):
        self.slots = {}

    def __getitem__(self, name):
        return self.slots.setdefault(name, len(self.slots))


def square(values):
    wide = values.astype(f32)
    return (wide * wide).astype(bf16)


def nt_dot(left, right):
    return lax.dot_general(
        left, right, (((1,), (1,)), ((), ())), preferred_element_type=f32
    )


def kernel(
    acts, grads, bin_t, bout_t, out,
    TB, CB, RO, SO, TH, CH, RT, ST, load_sem, send_sem, recv_sem,
):
    inb = lax.axis_index("inb")
    hid = lax.axis_index("hid")
    y, zl = inb // 4, inb % 4
    zh, x, c = hid // 8, (hid // 2) % 4, hid % 2

    is_mid = (zl == 1) | (zl == 2)

    def flip(value, mask):
        for bit in (1, 2):
            if mask & bit:
                value = value + bit - 2 * bit * ((value // bit) % 2)
        return value

    def peer(dy=0, dzl=0, dzh=0, dx=0, dc=0):
        return (
            flip(y, dy) * 4 + flip(zl, dzl),
            flip(zh, dzh) * 8 + flip(x, dx) * 2 + flip(c, dc),
        )

    slots, sends = Names(), []

    def send(name, ref, whom, target=None, when=None):
        copy = pltpu.make_async_remote_copy(
            ref, ref if target is None else target,
            send_sem.at[len(sends)], recv_sem.at[slots[name]],
            device_id=whom, device_id_type=MESH,
        )
        sends.append((copy, when))
        if when is None:
            copy.start()
        else:
            pl.when(when)(copy.start)

    def arrived(name, ref):
        pltpu.make_async_remote_copy(
            ref, ref, send_sem.at[0], recv_sem.at[slots[name]],
            device_id=peer(dc=1), device_id_type=MESH,
        ).wait_recv()

    def tb(dy, dzl, half):
        return TB.at[flip(zl, dzl) // 2, flip(y, dy) % 2, half]

    def cb(other, dzl, half):
        return CB.at[other, flip(zl, dzl) % 2, pl.ds(32 * half, 32)]

    def th(dzh, dx, half):
        return TH.at[flip(zh, dzh) % 2, flip(x, dx) % 2, c, half]

    def ch(other, dx, half):
        return CH.at[other, flip(x, dx) // 2, pl.ds(16 * half, 16)]

    def ro(dy, dzl, piece):
        yy, zz = flip(y, dy), flip(zl, dzl)
        return RO.at[2 * flip(yy, 3 * piece) + zz // 2, yy // 2, :, :, zz % 2]

    def rt(dzh, dx, piece):
        zz, ww = flip(zh, dzh), flip(x, dx)
        return RT.at[
            2 * (zz // 2) + ww // 2,
            flip(zz, 3 * piece),
            pl.ds(2 * ((ww // 2 + ww) % 2), 2),
            c,
        ]

    def rt_half(dzh, piece, group, dc=0):
        zz = flip(zh, dzh)
        return RT.at[2 * (zz // 2) + group, flip(zz, 3 * piece), :, flip(c, dc)]

    loads = [
        pltpu.make_async_copy(bout_t, CB.at[0, zl % 2], load_sem.at[0]),
        pltpu.make_async_copy(grads.at[:, pl.ds(0, 16)], tb(0, 0, 0), load_sem.at[1]),
        pltpu.make_async_copy(grads.at[:, pl.ds(16, 16)], tb(0, 0, 1), load_sem.at[2]),
        pltpu.make_async_copy(acts, TH.at[zh % 2, x % 2, c], load_sem.at[3]),
        pltpu.make_async_copy(bin_t, CH.at[0, x // 2], load_sem.at[4]),
    ]
    for load in loads:
        load.start()
    peers = [peer(dc=1)]
    peers += [peer(dx=d) for d in (1, 2, 3)]
    peers += [peer(dzh=d) for d in (1, 3)]
    peers += [peer(dy=d) for d in (1, 2, 3)]
    peers += [peer(dzl=d) for d in (1, 2, 3)]
    barrier = pltpu.get_barrier_semaphore()
    for whom in peers:
        pl.semaphore_signal(barrier, inc=1, device_id=whom, device_id_type=MESH)
    pl.semaphore_wait(barrier, len(peers))
    for load in loads:
        load.wait()

    for half in (0, 1):
        send(("Cz", half), cb(0, 0, half), peer(dzl=1))
        send(("Tz", half), tb(0, 0, half), peer(dzl=2))
    for half in (0, 1):
        send(("Cy", half), cb(0, 0, half), peer(dy=3), cb(1, 0, half))
        send(("Ty", half), tb(0, 0, half), peer(dy=1))
    for half in (0, 1):
        send(("tx", half), th(0, 0, half), peer(dx=1))
        send(("cx", half), ch(0, 0, half), peer(dx=3))
    for half in (0, 1):
        arrived(("Cz", half), cb(0, 1, half))
        send(("Cy2", half), cb(0, 1, half), peer(dy=3), cb(1, 1, half))
        arrived(("Tz", half), tb(0, 2, half))
        send(("Ty2", half), tb(0, 2, half), peer(dy=1))
    for half in (0, 1):
        send(("tz", half), th(0, 0, half), peer(dzh=1))
        send(("cz", half), ch(0, 0, half), peer(dzh=3), ch(1, 0, half))
    for half in (0, 1):
        arrived(("Ty", half), tb(1, 0, half))
        arrived(("Cy", half), cb(1, 0, half))
        arrived(("Ty2", half), tb(1, 2, half))
        arrived(("Cy2", half), cb(1, 1, half))

    def y_send(dzl):
        for piece, d in ((0, 3), (1, 3), (0, 1), (1, 1)):
            send(("Ry", dzl, piece, d), ro(0, dzl, piece), peer(dy=d))

    def y_direct(dzl):
        y_send(dzl)
        for piece in (0, 1):
            send(("Rr", dzl, piece), ro(0, dzl, piece), peer(dy=2))

    def y_relay(dzl):
        arrived(("Ry", dzl, 0, 1), ro(1, dzl, 0))
        send(("Rr", dzl, 0), ro(1, dzl, 0), peer(dy=3))
        arrived(("Ry", dzl, 1, 3), ro(3, dzl, 1))
        send(("Rr", dzl, 1), ro(3, dzl, 1), peer(dy=1))

    def z_wait(dzl):
        for piece in (0, 1):
            arrived(("Rz", dzl, piece), ro(0, dzl, piece))

    def x_send(dzh, piece):
        for d in (2, 1, 3):
            send(("rx", dzh, d, piece), rt(dzh, 0, piece), peer(dx=d))

    def core_send(dzh, *pieces):
        for piece in pieces:
            for d in (1, 3, 2):
                arrived(("rx", dzh, d, piece), rt(dzh, d, piece))
            for group in (0, 1):
                send(("rc", dzh, piece, group), rt_half(dzh, piece, group), peer(dc=1))

    def core_wait(dzh, *pieces):
        for piece in pieces:
            for group in (0, 1):
                arrived(("rc", dzh, piece, group), rt_half(dzh, piece, group, 1))

    tokens = TB[...].reshape(256, 1024)
    for piece in (0, 1):
        rotated = nt_dot(tokens, CB[piece].reshape(128, 1024)).astype(bf16)
        ro(0, 0, piece)[...] = rotated.reshape(2, 2, 64, 128)
    for d in (2, 1):
        for piece in (0, 1):
            send(("Rz", d, piece), ro(0, 0, piece), peer(dzl=d))
    for piece in (0, 1):
        send(("Rz", 3, piece), ro(0, 0, piece), peer(dzl=3), when=is_mid)
    y_send(0)
    for half in (0, 1):
        arrived(("tz", half), th(1, 0, half))
        send(("tx2", half), th(1, 0, half), peer(dx=1))
        arrived(("cz", half), ch(1, 0, half))
        send(("cx2", half), ch(1, 0, half), peer(dx=3))
    for half in (0, 1):
        arrived(("tx", half), th(0, 1, half))
        arrived(("cx", half), ch(0, 3, half))
    send("tc", TH.at[zh % 2, :, c], peer(dc=1))
    for half in (0, 1):
        arrived(("tx2", half), th(1, 1, half))
    send("tc2", TH.at[1 - zh % 2, :, c], peer(dc=1))
    for half in (0, 1):
        arrived(("cx2", half), ch(1, 3, half))
    z_wait(2)
    for piece in (0, 1):
        send(("Rz", 3, piece), ro(0, 2, piece), peer(dzl=1), when=is_mid)
    y_send(2)
    arrived("tc", TH.at[zh % 2, :, 1 - c])
    arrived("tc2", TH.at[1 - zh % 2, :, 1 - c])
    rotated = nt_dot(CH[...].reshape(128, 1024), TH[...].reshape(256, 1024)).astype(bf16)
    for piece in (0, 1):
        rt(0, 0, piece)[...] = rotated[64 * piece : 64 * piece + 64].reshape(2, 32, 256)
    for d, piece in ((1, 0), (3, 1), (1, 1), (3, 0)):
        send(("rz", d, piece), rt(0, 0, piece), peer(dzh=d))
    x_send(0, 0)
    x_send(0, 1)
    z_wait(1)
    y_send(1)
    y_relay(0)
    y_relay(2)
    y_relay(1)
    z_wait(3)
    y_direct(3)
    arrived(("rz", 1, 0), rt(1, 0, 0))
    send(("rr", 0), rt(1, 0, 0), peer(dzh=3))
    arrived(("rz", 3, 1), rt(3, 0, 1))
    send(("rr", 1), rt(3, 0, 1), peer(dzh=1))
    x_send(3, 1)
    arrived(("rz", 3, 0), rt(3, 0, 0))
    x_send(3, 0)
    x_send(1, 0)
    arrived(("rz", 1, 1), rt(1, 0, 1))
    x_send(1, 1)
    def square_rows(dzh):
        row = flip(zh, dzh)

        @pl.loop(0, 4)
        def _(group):
            ST[group, row] = square(RT[group, row])

    def square_columns(dy):
        first = 2 * flip(y, dy)

        @pl.loop(0, 2)
        def _(i):
            SO[first + i] = square(RO[first + i])

    def finish(dzh, dy):
        row, column = flip(zh, dzh), flip(y, dy)

        def left(ref):
            return jnp.concatenate(
                [ref[group, row].reshape(256, 256) for group in range(4)], axis=1
            )

        def right(ref):
            return jnp.concatenate(
                [ref[2 * column + i].reshape(1024, 128) for i in (0, 1)], axis=1
            )

        grad = jnp.dot(left(RT), right(RO), preferred_element_type=f32)
        fisher = jnp.dot(left(ST), right(SO), preferred_element_type=f32)
        result = (grad / (fisher + damping)).astype(bf16)
        lanes = pl.ds(pl.multiple_of(column * 256, 256), 256)
        for place, part in enumerate((0, 3, 1, 2)):
            rows = pl.ds(pl.multiple_of(row * 256 + 64 * part, 64), 64)
            out[rows, lanes] = result[64 * place : 64 * place + 64]

    core_send(0, 0, 1)
    for piece in (1, 0):
        arrived(("rr", piece), rt(2, 0, piece))
        x_send(2, piece)
    core_send(3, 1, 0)
    for dzl in (0, 1, 2, 3):
        arrived(("Ry", dzl, 0, 3), ro(3, dzl, 0))
    arrived(("Ry", 3, 1, 3), ro(3, 3, 1))
    square_columns(0)
    square_columns(3)
    for dzh in (0, 3):
        core_wait(dzh, 0, 1)
    for dzh in (0, 3):
        square_rows(dzh)
    finish(0, 0)
    finish(3, 0)
    core_send(1, 0, 1)
    finish(0, 3)
    finish(3, 3)
    core_send(2, 1)
    arrived(("Ry", 3, 0, 1), ro(1, 3, 0))
    for dzl in (0, 1, 2, 3):
        arrived(("Ry", dzl, 1, 1), ro(1, dzl, 1))
        arrived(("Rr", dzl, 0), ro(2, dzl, 0))
        arrived(("Rr", dzl, 1), ro(2, dzl, 1))
    square_columns(1)
    square_columns(2)
    finish(0, 1)
    finish(3, 1)
    core_send(2, 0)
    finish(0, 2)
    finish(3, 2)
    core_wait(1, 0)
    core_wait(2, 1)
    square_rows(1)
    for dy in (0, 3, 1, 2):
        finish(1, dy)
    core_wait(1, 1)
    core_wait(2, 0)
    square_rows(2)
    for dy in (0, 3, 1, 2):
        finish(2, dy)
    for copy, when in sends:
        if when is None:
            copy.wait_send()
        else:
            pl.when(when)(copy.wait_send)


def on_device(activations, out_grads, basis_in, basis_out):
    shards = (activations, out_grads, basis_in.T, basis_out.T)
    return pl.pallas_call(
        kernel,
        out_shape=jax.ShapeDtypeStruct((1024, 1024), bf16),
        in_specs=[pl.BlockSpec(memory_space=pltpu.HBM)] * 4,
        out_specs=pl.BlockSpec(memory_space=pltpu.VMEM),
        scratch_shapes=[
            pltpu.VMEM((2, 2, 2, 2, 16, 1024), bf16),
            pltpu.VMEM((2, 2, 64, 1024), bf16),
            pltpu.VMEM((8, 2, 2, 2, 2, 64, 128), bf16),
            pltpu.VMEM((8, 2, 2, 2, 2, 64, 128), bf16),
            pltpu.VMEM((2, 2, 2, 2, 16, 1024), bf16),
            pltpu.VMEM((2, 2, 32, 1024), bf16),
            pltpu.VMEM((4, 4, 4, 2, 32, 256), bf16),
            pltpu.VMEM((4, 4, 4, 2, 32, 256), bf16),
            pltpu.SemaphoreType.DMA((5,)),
            pltpu.SemaphoreType.DMA((128,)),
            pltpu.SemaphoreType.DMA((112,)),
        ],
        compiler_params=pltpu.CompilerParams(
            collective_id=0, has_side_effects=True, vmem_limit_bytes=48 * 2**20
        ),
        name="fused",
    )(*(pltpu.with_memory_space_constraint(shard, pltpu.HBM) for shard in shards))


def solution(mesh):
    return jax.shard_map(
        on_device,
        mesh=mesh,
        in_specs=(P(None, "hid", "inb"), P(None, "inb", "hid"), P("inb", "hid"), P("hid", "inb")),
        out_specs=P("inb", "hid"),
        check_vma=False,
    )
```

```python
import functools

import jax
import jax.numpy as jnp
from jax import lax
from jax.experimental import pallas as pl
from jax.experimental.pallas import tpu as pltpu
from jax.sharding import PartitionSpec as P

damping = 0.1
MESH = pl.DeviceIdType.MESH
bf16 = jnp.bfloat16
f32 = jnp.float32


class Names:
    def __init__(self):
        self.slots = {}

    def __getitem__(self, name):
        return self.slots.setdefault(name, len(self.slots))


def square(values):
    wide = values.astype(f32)
    return (wide * wide).astype(bf16)


def nt_dot(left, right):
    return lax.dot_general(
        left, right, (((1,), (1,)), ((), ())), preferred_element_type=f32
    )


def kernel(
    acts, grads, bin_t, bout_t, out,
    TB, CB, RO, SO, TH, CH, RT, ST, load_sem, send_sem, recv_sem,
):
    inb = lax.axis_index("inb")
    hid = lax.axis_index("hid")
    y, zl = inb // 4, inb % 4
    zh, x, c = hid // 8, (hid // 2) % 4, hid % 2

    is_mid = (zl == 1) | (zl == 2)

    def flip(value, mask):
        for bit in (1, 2):
            if mask & bit:
                value = value + bit - 2 * bit * ((value // bit) % 2)
        return value

    def peer(dy=0, dzl=0, dzh=0, dx=0, dc=0):
        return (
            flip(y, dy) * 4 + flip(zl, dzl),
            flip(zh, dzh) * 8 + flip(x, dx) * 2 + flip(c, dc),
        )

    slots, sends = Names(), []

    def send(name, ref, whom, target=None, when=None):
        copy = pltpu.make_async_remote_copy(
            ref, ref if target is None else target,
            send_sem.at[len(sends)], recv_sem.at[slots[name]],
            device_id=whom, device_id_type=MESH,
        )
        sends.append((copy, when))
        if when is None:
            copy.start()
        else:
            pl.when(when)(copy.start)

    def arrived(name, ref):
        pltpu.make_async_remote_copy(
            ref, ref, send_sem.at[0], recv_sem.at[slots[name]],
            device_id=peer(dc=1), device_id_type=MESH,
        ).wait_recv()

    def tb(dy, dzl, half):
        return TB.at[flip(zl, dzl) // 2, flip(y, dy) % 2, half]

    def cb(other, dzl, half):
        return CB.at[other, flip(zl, dzl) % 2, pl.ds(32 * half, 32)]

    def th(dzh, dx, half):
        return TH.at[flip(zh, dzh) % 2, flip(x, dx) % 2, c, half]

    def ch(other, dx, half):
        return CH.at[other, flip(x, dx) // 2, pl.ds(16 * half, 16)]

    def ro(dy, dzl, piece):
        yy, zz = flip(y, dy), flip(zl, dzl)
        return RO.at[2 * flip(yy, 3 * piece) + zz // 2, yy // 2, :, :, zz % 2]

    def rt(dzh, dx, piece):
        zz, ww = flip(zh, dzh), flip(x, dx)
        return RT.at[
            2 * (zz // 2) + ww // 2,
            flip(zz, 3 * piece),
            pl.ds(2 * ((ww // 2 + ww) % 2), 2),
            c,
        ]

    def rt_half(dzh, piece, group, dc=0):
        zz = flip(zh, dzh)
        return RT.at[2 * (zz // 2) + group, flip(zz, 3 * piece), :, flip(c, dc)]

    loads = [
        pltpu.make_async_copy(bout_t, CB.at[0, zl % 2], load_sem.at[0]),
        pltpu.make_async_copy(grads.at[:, pl.ds(0, 16)], tb(0, 0, 0), load_sem.at[1]),
        pltpu.make_async_copy(grads.at[:, pl.ds(16, 16)], tb(0, 0, 1), load_sem.at[2]),
        pltpu.make_async_copy(acts, TH.at[zh % 2, x % 2, c], load_sem.at[3]),
        pltpu.make_async_copy(bin_t, CH.at[0, x // 2], load_sem.at[4]),
    ]
    for load in loads:
        load.start()
    peers = [peer(dc=1)]
    peers += [peer(dx=d) for d in (1, 2, 3)]
    peers += [peer(dzh=d) for d in (1, 3)]
    peers += [peer(dy=d) for d in (1, 2, 3)]
    peers += [peer(dzl=d) for d in (1, 2, 3)]
    barrier = pltpu.get_barrier_semaphore()
    for whom in peers:
        pl.semaphore_signal(barrier, inc=1, device_id=whom, device_id_type=MESH)
    pl.semaphore_wait(barrier, len(peers))
    for load in loads:
        load.wait()

    for half in (0, 1):
        send(("Cz", half), cb(0, 0, half), peer(dzl=1))
        send(("Tz", half), tb(0, 0, half), peer(dzl=2))
    for half in (0, 1):
        send(("Cy", half), cb(0, 0, half), peer(dy=3), cb(1, 0, half))
        send(("Ty", half), tb(0, 0, half), peer(dy=1))
    for half in (0, 1):
        send(("tx", half), th(0, 0, half), peer(dx=1))
        send(("cx", half), ch(0, 0, half), peer(dx=3))
    for half in (0, 1):
        arrived(("Cz", half), cb(0, 1, half))
        send(("Cy2", half), cb(0, 1, half), peer(dy=3), cb(1, 1, half))
        arrived(("Tz", half), tb(0, 2, half))
        send(("Ty2", half), tb(0, 2, half), peer(dy=1))
        send(("tz", half), th(0, 0, half), peer(dzh=1))
        send(("cz", half), ch(0, 0, half), peer(dzh=3), ch(1, 0, half))
    for half in (0, 1):
        arrived(("Ty", half), tb(1, 0, half))
        arrived(("Cy", half), cb(1, 0, half))
        arrived(("Ty2", half), tb(1, 2, half))
        arrived(("Cy2", half), cb(1, 1, half))

    def y_send(dzl):
        for piece, d in ((0, 3), (1, 3), (0, 1), (1, 1)):
            send(("Ry", dzl, piece, d), ro(0, dzl, piece), peer(dy=d))

    def y_direct(dzl):
        y_send(dzl)
        for piece in (0, 1):
            send(("Rr", dzl, piece), ro(0, dzl, piece), peer(dy=2))

    def y_relay(dzl):
        arrived(("Ry", dzl, 0, 1), ro(1, dzl, 0))
        send(("Rr", dzl, 0), ro(1, dzl, 0), peer(dy=3))
        arrived(("Ry", dzl, 1, 3), ro(3, dzl, 1))
        send(("Rr", dzl, 1), ro(3, dzl, 1), peer(dy=1))

    def z_wait(dzl):
        for piece in (0, 1):
            arrived(("Rz", dzl, piece), ro(0, dzl, piece))

    def x_send(dzh, piece):
        for d in (2, 1, 3):
            send(("rx", dzh, d, piece), rt(dzh, 0, piece), peer(dx=d))

    def core_send(dzh, *pieces):
        for piece in pieces:
            for d in (1, 3, 2):
                arrived(("rx", dzh, d, piece), rt(dzh, d, piece))
            for group in (0, 1):
                send(("rc", dzh, piece, group), rt_half(dzh, piece, group), peer(dc=1))

    def core_wait(dzh, *pieces):
        for piece in pieces:
            for group in (0, 1):
                arrived(("rc", dzh, piece, group), rt_half(dzh, piece, group, 1))

    tokens = TB[...].reshape(256, 1024)
    for piece in (0, 1):
        rotated = nt_dot(tokens, CB[piece].reshape(128, 1024)).astype(bf16)
        ro(0, 0, piece)[...] = rotated.reshape(2, 2, 64, 128)
    for d in (2, 1):
        for piece in (0, 1):
            send(("Rz", d, piece), ro(0, 0, piece), peer(dzl=d))
    for piece in (0, 1):
        send(("Rz", 3, piece), ro(0, 0, piece), peer(dzl=3), when=is_mid)
    y_send(0)
    for half in (0, 1):
        arrived(("tz", half), th(1, 0, half))
        send(("tx2", half), th(1, 0, half), peer(dx=1))
        arrived(("cz", half), ch(1, 0, half))
        send(("cx2", half), ch(1, 0, half), peer(dx=3))
    for half in (0, 1):
        arrived(("tx", half), th(0, 1, half))
        arrived(("cx", half), ch(0, 3, half))
    send("tc", TH.at[zh % 2, :, c], peer(dc=1))
    for half in (0, 1):
        arrived(("tx2", half), th(1, 1, half))
    send("tc2", TH.at[1 - zh % 2, :, c], peer(dc=1))
    for half in (0, 1):
        arrived(("cx2", half), ch(1, 3, half))
    z_wait(2)
    for piece in (0, 1):
        send(("Rz", 3, piece), ro(0, 2, piece), peer(dzl=1), when=is_mid)
    y_send(2)
    arrived("tc", TH.at[zh % 2, :, 1 - c])
    arrived("tc2", TH.at[1 - zh % 2, :, 1 - c])
    rotated = nt_dot(CH[...].reshape(128, 1024), TH[...].reshape(256, 1024)).astype(bf16)
    for piece in (0, 1):
        rt(0, 0, piece)[...] = rotated[64 * piece : 64 * piece + 64].reshape(2, 32, 256)
    for d, piece in ((1, 0), (3, 1), (1, 1), (3, 0)):
        send(("rz", d, piece), rt(0, 0, piece), peer(dzh=d))
    x_send(0, 0)
    x_send(0, 1)
    z_wait(1)
    y_send(1)
    y_relay(0)
    y_relay(2)
    y_relay(1)
    z_wait(3)
    y_direct(3)
    arrived(("rz", 1, 0), rt(1, 0, 0))
    send(("rr", 0), rt(1, 0, 0), peer(dzh=3))
    arrived(("rz", 3, 1), rt(3, 0, 1))
    send(("rr", 1), rt(3, 0, 1), peer(dzh=1))
    x_send(3, 1)
    arrived(("rz", 3, 0), rt(3, 0, 0))
    x_send(3, 0)
    x_send(1, 0)
    arrived(("rz", 1, 1), rt(1, 0, 1))
    x_send(1, 1)
    def square_rows(dzh, core):
        row = flip(zh, dzh)

        @pl.loop(0, 4)
        def _(group):
            ST[group, row, :, core] = square(RT[group, row, :, core])

    def square_columns(dy):
        first = 2 * flip(y, dy)

        @pl.loop(0, 2)
        def _(i):
            SO[first + i] = square(RO[first + i])

    def finish(dzh, dy):
        row, column = flip(zh, dzh), flip(y, dy)

        def left(ref):
            return jnp.concatenate(
                [ref[group, row].reshape(256, 256) for group in range(4)], axis=1
            )

        def right(ref):
            return jnp.concatenate(
                [ref[2 * column + i].reshape(1024, 128) for i in (0, 1)], axis=1
            )

        grad = jnp.dot(left(RT), right(RO), preferred_element_type=f32)
        fisher = jnp.dot(left(ST), right(SO), preferred_element_type=f32)
        result = (grad / (fisher + damping)).astype(bf16)
        lanes = pl.ds(pl.multiple_of(column * 256, 256), 256)
        for place, part in enumerate((0, 3, 1, 2)):
            rows = pl.ds(pl.multiple_of(row * 256 + 64 * part, 64), 64)
            out[rows, lanes] = result[64 * place : 64 * place + 64]

    core_send(0, 0, 1)
    core_send(3, 1, 0)
    for piece in (1, 0):
        arrived(("rr", piece), rt(2, 0, piece))
        x_send(2, piece)
    for dzh in (0, 3):
        square_rows(dzh, c)
    for dzl in (0, 1, 2, 3):
        arrived(("Ry", dzl, 0, 3), ro(3, dzl, 0))
    arrived(("Ry", 3, 1, 3), ro(3, 3, 1))
    square_columns(0)
    square_columns(3)
    for dzh in (0, 3):
        core_wait(dzh, 0, 1)
    for dzh in (0, 3):
        square_rows(dzh, 1 - c)
    finish(0, 0)
    finish(3, 0)
    core_send(1, 0, 1)
    finish(0, 3)
    finish(3, 3)
    core_send(2, 1)
    arrived(("Ry", 3, 0, 1), ro(1, 3, 0))
    for dzl in (0, 1, 2, 3):
        arrived(("Ry", dzl, 1, 1), ro(1, dzl, 1))
        arrived(("Rr", dzl, 0), ro(2, dzl, 0))
        arrived(("Rr", dzl, 1), ro(2, dzl, 1))
    square_columns(1)
    square_columns(2)
    finish(0, 1)
    finish(3, 1)
    core_send(2, 0)
    finish(0, 2)
    finish(3, 2)
    core_wait(1, 0)
    core_wait(2, 1)
    square_rows(1, c)
    square_rows(1, 1 - c)
    for dy in (0, 3, 1, 2):
        finish(1, dy)
    core_wait(1, 1)
    core_wait(2, 0)
    square_rows(2, c)
    square_rows(2, 1 - c)
    for dy in (0, 3, 1, 2):
        finish(2, dy)
    for copy, when in sends:
        if when is None:
            copy.wait_send()
        else:
            pl.when(when)(copy.wait_send)


def on_device(activations, out_grads, basis_in, basis_out):
    shards = (activations, out_grads, basis_in.T, basis_out.T)
    return pl.pallas_call(
        kernel,
        out_shape=jax.ShapeDtypeStruct((1024, 1024), bf16),
        in_specs=[pl.BlockSpec(memory_space=pltpu.HBM)] * 4,
        out_specs=pl.BlockSpec(memory_space=pltpu.VMEM),
        scratch_shapes=[
            pltpu.VMEM((2, 2, 2, 2, 16, 1024), bf16),
            pltpu.VMEM((2, 2, 64, 1024), bf16),
            pltpu.VMEM((8, 2, 2, 2, 2, 64, 128), bf16),
            pltpu.VMEM((8, 2, 2, 2, 2, 64, 128), bf16),
            pltpu.VMEM((2, 2, 2, 2, 16, 1024), bf16),
            pltpu.VMEM((2, 2, 32, 1024), bf16),
            pltpu.VMEM((4, 4, 4, 2, 32, 256), bf16),
            pltpu.VMEM((4, 4, 4, 2, 32, 256), bf16),
            pltpu.SemaphoreType.DMA((5,)),
            pltpu.SemaphoreType.DMA((128,)),
            pltpu.SemaphoreType.DMA((112,)),
        ],
        compiler_params=pltpu.CompilerParams(
            collective_id=0, has_side_effects=True, vmem_limit_bytes=48 * 2**20
        ),
        name="fused",
    )(*(pltpu.with_memory_space_constraint(shard, pltpu.HBM) for shard in shards))


def solution(mesh):
    return jax.shard_map(
        on_device,
        mesh=mesh,
        in_specs=(P(None, "hid", "inb"), P(None, "inb", "hid"), P("inb", "hid"), P("hid", "inb")),
        out_specs=P("inb", "hid"),
        check_vma=False,
    )
```

```python
import functools

import jax
import jax.numpy as jnp
from jax import lax
from jax.experimental import pallas as pl
from jax.experimental.pallas import tpu as pltpu
from jax.sharding import PartitionSpec as P

damping = 0.1
MESH = pl.DeviceIdType.MESH
bf16 = jnp.bfloat16
f32 = jnp.float32


class Names:
    def __init__(self):
        self.slots = {}

    def __getitem__(self, name):
        return self.slots.setdefault(name, len(self.slots))


def square(values):
    wide = values.astype(f32)
    return (wide * wide).astype(bf16)


def nt_dot(left, right):
    return lax.dot_general(
        left, right, (((1,), (1,)), ((), ())), preferred_element_type=f32
    )


def kernel(
    acts, grads, bin_t, bout_t, out,
    TB, CB, RO, SO, TH, CH, RT, ST, load_sem, send_sem, recv_sem,
):
    inb = lax.axis_index("inb")
    hid = lax.axis_index("hid")
    y, zl = inb // 4, inb % 4
    zh, x, c = hid // 8, (hid // 2) % 4, hid % 2

    is_mid = (zl == 1) | (zl == 2)

    def flip(value, mask):
        for bit in (1, 2):
            if mask & bit:
                value = value + bit - 2 * bit * ((value // bit) % 2)
        return value

    def peer(dy=0, dzl=0, dzh=0, dx=0, dc=0):
        return (
            flip(y, dy) * 4 + flip(zl, dzl),
            flip(zh, dzh) * 8 + flip(x, dx) * 2 + flip(c, dc),
        )

    slots, sends = Names(), []

    def send(name, ref, whom, target=None, when=None):
        copy = pltpu.make_async_remote_copy(
            ref, ref if target is None else target,
            send_sem.at[len(sends)], recv_sem.at[slots[name]],
            device_id=whom, device_id_type=MESH,
        )
        sends.append((copy, when))
        if when is None:
            copy.start()
        else:
            pl.when(when)(copy.start)

    def arrived(name, ref):
        pltpu.make_async_remote_copy(
            ref, ref, send_sem.at[0], recv_sem.at[slots[name]],
            device_id=peer(dc=1), device_id_type=MESH,
        ).wait_recv()

    def tb(dy, dzl, half):
        return TB.at[flip(zl, dzl) // 2, flip(y, dy) % 2, half]

    def cb(other, dzl, half):
        return CB.at[other, flip(zl, dzl) % 2, pl.ds(32 * half, 32)]

    def th(dzh, dx, half):
        return TH.at[flip(zh, dzh) % 2, flip(x, dx) % 2, c, half]

    def ch(other, dx, half):
        return CH.at[other, flip(x, dx) // 2, pl.ds(16 * half, 16)]

    def ro(dy, dzl, piece):
        yy, zz = flip(y, dy), flip(zl, dzl)
        return RO.at[2 * flip(yy, 3 * piece) + zz // 2, yy // 2, :, :, zz % 2]

    def rt(dzh, dx, piece):
        zz, ww = flip(zh, dzh), flip(x, dx)
        return RT.at[
            2 * (zz // 2) + ww // 2,
            flip(zz, 3 * piece),
            pl.ds(2 * ((ww // 2 + ww) % 2), 2),
            c,
        ]

    def rt_half(dzh, piece, group, dc=0):
        zz = flip(zh, dzh)
        return RT.at[2 * (zz // 2) + group, flip(zz, 3 * piece), :, flip(c, dc)]

    loads = [
        pltpu.make_async_copy(bout_t, CB.at[0, zl % 2], load_sem.at[0]),
        pltpu.make_async_copy(grads.at[:, pl.ds(0, 16)], tb(0, 0, 0), load_sem.at[1]),
        pltpu.make_async_copy(grads.at[:, pl.ds(16, 16)], tb(0, 0, 1), load_sem.at[2]),
        pltpu.make_async_copy(acts, TH.at[zh % 2, x % 2, c], load_sem.at[3]),
        pltpu.make_async_copy(bin_t, CH.at[0, x // 2], load_sem.at[4]),
    ]
    for load in loads:
        load.start()
    peers = [peer(dc=1)]
    peers += [peer(dx=d) for d in (1, 2, 3)]
    peers += [peer(dzh=d) for d in (1, 3)]
    peers += [peer(dy=d) for d in (1, 2, 3)]
    peers += [peer(dzl=d) for d in (1, 2, 3)]
    barrier = pltpu.get_barrier_semaphore()
    for whom in peers:
        pl.semaphore_signal(barrier, inc=1, device_id=whom, device_id_type=MESH)
    pl.semaphore_wait(barrier, len(peers))
    for load in loads:
        load.wait()

    for half in (0, 1):
        send(("Tz", half), tb(0, 0, half), peer(dzl=2))
        send(("Cz", half), cb(0, 0, half), peer(dzl=1))
    for half in (0, 1):
        send(("Cy", half), cb(0, 0, half), peer(dy=3), cb(1, 0, half))
        send(("Ty", half), tb(0, 0, half), peer(dy=1))
    for half in (0, 1):
        send(("tx", half), th(0, 0, half), peer(dx=1))
        send(("cx", half), ch(0, 0, half), peer(dx=3))
    for half in (0, 1):
        arrived(("Cz", half), cb(0, 1, half))
        send(("Cy2", half), cb(0, 1, half), peer(dy=3), cb(1, 1, half))
        arrived(("Tz", half), tb(0, 2, half))
        send(("Ty2", half), tb(0, 2, half), peer(dy=1))
        send(("tz", half), th(0, 0, half), peer(dzh=1))
        send(("cz", half), ch(0, 0, half), peer(dzh=3), ch(1, 0, half))
    for half in (0, 1):
        arrived(("Ty", half), tb(1, 0, half))
        arrived(("Cy", half), cb(1, 0, half))
        arrived(("Ty2", half), tb(1, 2, half))
        arrived(("Cy2", half), cb(1, 1, half))

    def y_send(dzl):
        for piece, d in ((0, 3), (1, 3), (0, 1), (1, 1)):
            send(("Ry", dzl, piece, d), ro(0, dzl, piece), peer(dy=d))

    def y_direct(dzl):
        y_send(dzl)
        for piece in (0, 1):
            send(("Rr", dzl, piece), ro(0, dzl, piece), peer(dy=2))

    def y_relay(dzl):
        arrived(("Ry", dzl, 0, 1), ro(1, dzl, 0))
        send(("Rr", dzl, 0), ro(1, dzl, 0), peer(dy=3))
        arrived(("Ry", dzl, 1, 3), ro(3, dzl, 1))
        send(("Rr", dzl, 1), ro(3, dzl, 1), peer(dy=1))

    def z_wait(dzl):
        for piece in (0, 1):
            arrived(("Rz", dzl, piece), ro(0, dzl, piece))

    def x_send(dzh, piece):
        for d in (2, 1, 3):
            send(("rx", dzh, d, piece), rt(dzh, 0, piece), peer(dx=d))

    def core_send(dzh, *pieces):
        for piece in pieces:
            for d in (1, 3, 2):
                arrived(("rx", dzh, d, piece), rt(dzh, d, piece))
            for group in (0, 1):
                send(("rc", dzh, piece, group), rt_half(dzh, piece, group), peer(dc=1))

    def core_wait(dzh, *pieces):
        for piece in pieces:
            for group in (0, 1):
                arrived(("rc", dzh, piece, group), rt_half(dzh, piece, group, 1))

    tokens = TB[...].reshape(256, 1024)
    for piece in (0, 1):
        rotated = nt_dot(tokens, CB[piece].reshape(128, 1024)).astype(bf16)
        ro(0, 0, piece)[...] = rotated.reshape(2, 2, 64, 128)
    for d in (2, 1):
        for piece in (0, 1):
            send(("Rz", d, piece), ro(0, 0, piece), peer(dzl=d))
    for piece in (0, 1):
        send(("Rz", 3, piece), ro(0, 0, piece), peer(dzl=3), when=is_mid)
    y_send(0)
    for half in (0, 1):
        arrived(("tz", half), th(1, 0, half))
        send(("tx2", half), th(1, 0, half), peer(dx=1))
        arrived(("cz", half), ch(1, 0, half))
        send(("cx2", half), ch(1, 0, half), peer(dx=3))
    for half in (0, 1):
        arrived(("tx", half), th(0, 1, half))
        arrived(("cx", half), ch(0, 3, half))
    send("tc", TH.at[zh % 2, :, c], peer(dc=1))
    for half in (0, 1):
        arrived(("tx2", half), th(1, 1, half))
    send("tc2", TH.at[1 - zh % 2, :, c], peer(dc=1))
    for half in (0, 1):
        arrived(("cx2", half), ch(1, 3, half))
    z_wait(2)
    for piece in (0, 1):
        send(("Rz", 3, piece), ro(0, 2, piece), peer(dzl=1), when=is_mid)
    y_send(2)
    arrived("tc", TH.at[zh % 2, :, 1 - c])
    arrived("tc2", TH.at[1 - zh % 2, :, 1 - c])
    rotated = nt_dot(CH[...].reshape(128, 1024), TH[...].reshape(256, 1024)).astype(bf16)
    for piece in (0, 1):
        rt(0, 0, piece)[...] = rotated[64 * piece : 64 * piece + 64].reshape(2, 32, 256)
    for d, piece in ((1, 0), (3, 1), (1, 1), (3, 0)):
        send(("rz", d, piece), rt(0, 0, piece), peer(dzh=d))
    x_send(0, 0)
    x_send(0, 1)
    z_wait(1)
    y_send(1)
    y_relay(0)
    y_relay(2)
    y_relay(1)
    z_wait(3)
    y_direct(3)
    arrived(("rz", 1, 0), rt(1, 0, 0))
    send(("rr", 0), rt(1, 0, 0), peer(dzh=3))
    arrived(("rz", 3, 1), rt(3, 0, 1))
    send(("rr", 1), rt(3, 0, 1), peer(dzh=1))
    x_send(3, 1)
    arrived(("rz", 3, 0), rt(3, 0, 0))
    x_send(3, 0)
    x_send(1, 0)
    arrived(("rz", 1, 1), rt(1, 0, 1))
    x_send(1, 1)
    def square_rows(dzh, core):
        row = flip(zh, dzh)

        @pl.loop(0, 4)
        def _(group):
            ST[group, row, :, core] = square(RT[group, row, :, core])

    def square_columns(dy):
        first = 2 * flip(y, dy)

        @pl.loop(0, 2)
        def _(i):
            SO[first + i] = square(RO[first + i])

    def finish(dzh, dy):
        row, column = flip(zh, dzh), flip(y, dy)

        def left(ref):
            return jnp.concatenate(
                [
                    jnp.concatenate(
                        [ref[group, row, place].reshape(64, 256) for place in (0, 2, 3, 1)],
                        axis=0,
                    )
                    for group in range(4)
                ],
                axis=1,
            )

        def right(ref):
            return jnp.concatenate(
                [ref[2 * column + i].reshape(1024, 128) for i in (0, 1)], axis=1
            )

        grad = jnp.dot(left(RT), right(RO), preferred_element_type=f32)
        fisher = jnp.dot(left(ST), right(SO), preferred_element_type=f32)
        out[
            pl.ds(pl.multiple_of(row * 256, 256), 256),
            pl.ds(pl.multiple_of(column * 256, 256), 256),
        ] = (grad / (fisher + damping)).astype(bf16)

    core_send(0, 0, 1)
    core_send(3, 1, 0)
    for piece in (1, 0):
        arrived(("rr", piece), rt(2, 0, piece))
        x_send(2, piece)
    for dzh in (0, 3):
        square_rows(dzh, c)
    for dzl in (0, 1, 2, 3):
        arrived(("Ry", dzl, 0, 3), ro(3, dzl, 0))
    arrived(("Ry", 3, 1, 3), ro(3, 3, 1))
    square_columns(0)
    square_columns(3)
    for dzh in (0, 3):
        core_wait(dzh, 0, 1)
    for dzh in (0, 3):
        square_rows(dzh, 1 - c)
    finish(0, 0)
    finish(3, 0)
    core_send(1, 0, 1)
    finish(0, 3)
    finish(3, 3)
    core_send(2, 1)
    arrived(("Ry", 3, 0, 1), ro(1, 3, 0))
    for dzl in (0, 1, 2, 3):
        arrived(("Ry", dzl, 1, 1), ro(1, dzl, 1))
        arrived(("Rr", dzl, 0), ro(2, dzl, 0))
        arrived(("Rr", dzl, 1), ro(2, dzl, 1))
    square_columns(1)
    square_columns(2)
    finish(0, 1)
    finish(3, 1)
    core_send(2, 0)
    finish(0, 2)
    finish(3, 2)
    core_wait(1, 0)
    core_wait(2, 1)
    square_rows(1, c)
    square_rows(1, 1 - c)
    for dy in (0, 3, 1, 2):
        finish(1, dy)
    core_wait(1, 1)
    core_wait(2, 0)
    square_rows(2, c)
    square_rows(2, 1 - c)
    for dy in (0, 3, 1, 2):
        finish(2, dy)
    for copy, when in sends:
        if when is None:
            copy.wait_send()
        else:
            pl.when(when)(copy.wait_send)


def on_device(activations, out_grads, basis_in, basis_out):
    shards = (activations, out_grads, basis_in.T, basis_out.T)
    return pl.pallas_call(
        kernel,
        out_shape=jax.ShapeDtypeStruct((1024, 1024), bf16),
        in_specs=[pl.BlockSpec(memory_space=pltpu.HBM)] * 4,
        out_specs=pl.BlockSpec(memory_space=pltpu.VMEM),
        scratch_shapes=[
            pltpu.VMEM((2, 2, 2, 2, 16, 1024), bf16),
            pltpu.VMEM((2, 2, 64, 1024), bf16),
            pltpu.VMEM((8, 2, 2, 2, 2, 64, 128), bf16),
            pltpu.VMEM((8, 2, 2, 2, 2, 64, 128), bf16),
            pltpu.VMEM((2, 2, 2, 2, 16, 1024), bf16),
            pltpu.VMEM((2, 2, 32, 1024), bf16),
            pltpu.VMEM((4, 4, 4, 2, 32, 256), bf16),
            pltpu.VMEM((4, 4, 4, 2, 32, 256), bf16),
            pltpu.SemaphoreType.DMA((5,)),
            pltpu.SemaphoreType.DMA((128,)),
            pltpu.SemaphoreType.DMA((112,)),
        ],
        compiler_params=pltpu.CompilerParams(
            collective_id=0, has_side_effects=True, vmem_limit_bytes=48 * 2**20
        ),
        name="fused",
    )(*(pltpu.with_memory_space_constraint(shard, pltpu.HBM) for shard in shards))


def solution(mesh):
    return jax.shard_map(
        on_device,
        mesh=mesh,
        in_specs=(P(None, "hid", "inb"), P(None, "inb", "hid"), P("inb", "hid"), P("hid", "inb")),
        out_specs=P("inb", "hid"),
        check_vma=False,
    )
```
